512 devices in a mesh: dp: 16 (over y, core), expert: 32 (over z, x).
Axes of the slice: x: 4, y: 8, z: 8, core: 2. Of those that a mesh axis runs over, the one named last changes fastest.
Arguments:
- tokens: bfloat16 [65536, 2048], P(('dp', 'expert')), may hold values from -6 to 6
- out_grad: bfloat16 [65536, 2048], P(('dp', 'expert')), may hold values from -6 to 6
- route_ids: int32 [65536, 2], P(('dp', 'expert')), may hold values from 0 to 31, as said below
- route_gates: bfloat16 [65536, 2], P(('dp', 'expert')), may hold values from 0.049804688 to 1
- weight_in: bfloat16 [32, 2048, 512], P('expert', 'dp'), may hold values from -0.125 to 0.125
- weight_out: bfloat16 [32, 512, 2048], P('expert', None, 'dp'), may hold values from -0.25 to 0.25
Outputs:
- grad_tokens: bfloat16 [65536, 2048], P(('dp', 'expert'))
- grad_gates: bfloat16 [65536, 2], P(('dp', 'expert'))
- grad_weight_in: float32 [32, 2048, 512], P('expert', 'dp')
- grad_weight_out: float32 [32, 512, 2048], P('expert', None, 'dp')
The draws below stay inside these ranges and needn't reach their ends.
Inputs may be any that keep to these rules, and one draw needn't show every extreme that they name: `route_ids`: each row names two different experts. Within the 128 tokens of one device (aligned blocks of 128 rows), every expert is named by at most 16 rows. For each index of dp, one expert is named by exactly 16 rows in every block of that index's 4096 rows.
All inputs are finite; a program needn't handle non-finite values.
Results may differ from the reference program's by a relative error of at most 0.017.
Values may be sent and summed in bfloat16 or wider, within the bound.
A program may use at most 64 MiB of HBM per device.

```python
import jax
import jax.numpy as jnp
from jax import lax

D = 2048
H = 512
TOK_DEV = 128
EXPERTS = 32
CAP = 16
TOKENS = 65536
N_DP = 16
N_EXPERT = 32


def draw_route_ids(key, part):
    blocks = N_DP * N_EXPERT
    capacity = 4 * TOK_DEV // N_EXPERT
    half_experts = N_EXPERT // 2
    jitter_width = capacity // 8
    row_keys = jax.random.split(jax.random.fold_in(key, 11), N_DP)

    def row_plan(row_key):
        expert_order = jax.random.permutation(jax.random.fold_in(row_key, 1), N_EXPERT).astype(jnp.int32)
        base_split = jax.random.randint(jax.random.fold_in(row_key, 2), (half_experts,), 0, capacity + 1)
        base_split = base_split.at[0].set(capacity)
        return (expert_order, base_split.astype(jnp.int32))
    orders, bases = jax.vmap(row_plan)(row_keys)
    device_keys = jax.random.split(jax.random.fold_in(key, 12), blocks)

    def block_ids(device_key, expert_order, base_split):
        jitter = jax.random.randint(jax.random.fold_in(device_key, 1), (half_experts,), -jitter_width, jitter_width + 1)
        jitter = jitter.at[0].set(0)
        split_count = jnp.clip(base_split + jitter.astype(jnp.int32), 0, capacity)
        count_by_rank = jnp.concatenate([split_count, capacity - split_count])
        counts = jnp.zeros((N_EXPERT,), jnp.int32).at[expert_order].set(count_by_rank)
        count_ends = jnp.cumsum(counts)
        position = jnp.arange(2 * TOK_DEV, dtype=jnp.int32)
        labels = jnp.sum((position[:, None] >= count_ends[None, :]).astype(jnp.int32), axis=1)
        pair_ids = jnp.stack([labels[:TOK_DEV], labels[TOK_DEV:]], axis=1)
        swap_bits = jax.random.randint(jax.random.fold_in(device_key, 3), (TOK_DEV, 1), 0, 2)
        pair_ids = jnp.where(swap_bits > 0, pair_ids[:, ::-1], pair_ids)
        row_order = jax.random.permutation(jax.random.fold_in(device_key, 2), TOK_DEV)
        return pair_ids[row_order]
    order_rep = jnp.repeat(orders, N_EXPERT, axis=0)
    base_rep = jnp.repeat(bases, N_EXPERT, axis=0)
    all_ids = jax.vmap(block_ids)(device_keys, order_rep, base_rep)
    return all_ids.reshape(TOKENS, 2).astype(jnp.int32)


def block_scale(rng, shape, cuts, smallest, top_value):
    factor_of = 1.0
    for dim, shards_of in cuts:
        draws = jax.random.uniform(jax.random.fold_in(jax.random.fold_in(rng, 6), dim), (shards_of,), jnp.float32, smallest / len(cuts), top_value / len(cuts))
        factor_of = factor_of * jnp.repeat(jnp.exp(draws), shape[dim] // shards_of).reshape((-1,) + (1,) * (len(shape) - 1 - dim))
    return factor_of


def centred(own_key, shape, spread, limit, cuts=(), kind=jnp.bfloat16):
    gain = block_scale(own_key, shape, cuts, -0.22, 0.18) if cuts else 1.0
    values = jax.random.normal(own_key, shape, jnp.float32) * spread * gain
    return jnp.minimum(jnp.maximum(values, -limit), limit).astype(kind)


def setup_inputs(seed: int = 0) -> dict:
    seeds = jax.random.split(jax.random.key(seed), 7)
    return {
        "tokens": centred(seeds[0], (TOKENS, D), 1.0, 6.0, ((0, 512),)),
        "out_grad": centred(seeds[1], (TOKENS, D), 1.0, 6.0, ((0, 512),)),
        "route_ids": draw_route_ids(jax.random.fold_in(seeds[6], 71), 0),
        "route_gates": jnp.clip(0.049804688 + 0.9501953 * jax.random.uniform(seeds[3], (TOKENS, 2), jnp.float32) ** block_scale(seeds[3], (TOKENS, 2), ((0, 512),), -0.2, 0.2), 0.049804688, 1.0).astype(jnp.bfloat16),
        "weight_in": centred(seeds[4], (EXPERTS, D, H), D ** -0.5, 0.125, ((0, 32), (1, 16))),
        "weight_out": centred(seeds[5], (EXPERTS, H, D), H ** -0.5, 0.25, ((0, 32), (2, 16))),
    }


def silu_slope(preact):
    logistic = jax.nn.sigmoid(preact)
    return logistic * (1.0 + preact * (1.0 - logistic))


def reference(tokens, out_grad, route_ids, route_gates, weight_in, weight_out):
    experts = weight_in.shape[0]
    blocks = N_DP * N_EXPERT
    capacity = CAP
    routes = 2 * TOKENS
    block_ids = route_ids.reshape(blocks, 2 * TOK_DEV).astype(jnp.int32)
    onehot = (block_ids[:, :, None] == jnp.arange(experts, dtype=jnp.int32)[None, None, :]).astype(jnp.int32)
    route_rank = jnp.sum(jnp.cumsum(onehot, axis=1) * onehot, axis=2) - 1
    block_number = jnp.arange(blocks, dtype=jnp.int32)[:, None]
    position = ((block_ids * blocks + block_number) * capacity + route_rank).reshape(-1).astype(jnp.int32)
    slot_table = jnp.full((experts * blocks * capacity,), routes, jnp.int32)
    slot_table = slot_table.at[position].set(jnp.arange(routes, dtype=jnp.int32))
    slot_table = slot_table.reshape(experts, N_DP, N_EXPERT * capacity)
    gate_flat = route_gates.reshape(-1)
    group_shape = (N_DP, N_EXPERT * capacity)

    def one_expert(loop_state, expert_data):
        token_sum, gate_out = loop_state
        expert_rows, proj_in, proj_out = expert_data
        flat_rows = expert_rows.reshape(-1)
        token_index = (flat_rows // 2).astype(jnp.int32)
        inputs = jnp.take(tokens, token_index, axis=0, mode="fill", fill_value=0)
        grad_rows = jnp.take(out_grad, token_index, axis=0, mode="fill", fill_value=0)
        gate_rows = jnp.take(gate_flat, flat_rows, axis=0, mode="fill", fill_value=0)
        preact = jnp.dot(inputs, proj_in, preferred_element_type=jnp.float32)
        hidden_act = jax.nn.silu(preact).astype(jnp.bfloat16)
        back_grad = jnp.dot(grad_rows, proj_out.T, preferred_element_type=jnp.float32)
        weight = gate_rows.astype(jnp.float32)[:, None]
        gate_grad = jnp.sum(hidden_act.astype(jnp.float32) * back_grad, axis=1).astype(jnp.bfloat16)
        pre_grad = (weight * back_grad * silu_slope(preact)).astype(jnp.bfloat16)
        scaled = (weight * grad_rows.astype(jnp.float32)).astype(jnp.bfloat16)
        route_grad = jnp.dot(pre_grad, proj_in.T, preferred_element_type=jnp.float32).astype(jnp.bfloat16)
        token_sum = token_sum.at[token_index].add(route_grad.astype(token_sum.dtype), mode="drop")
        gate_out = gate_out.at[flat_rows].set(gate_grad, mode="drop")
        width = inputs.shape[1]
        hidden = preact.shape[1]
        part_in = jnp.einsum("gsd,gsh->gdh", inputs.reshape(group_shape + (width,)).astype(jnp.float32),
                             pre_grad.reshape(group_shape + (hidden,)).astype(jnp.float32)).astype(jnp.bfloat16)
        part_out = jnp.einsum("gsh,gsd->ghd", hidden_act.reshape(group_shape + (hidden,)).astype(jnp.float32),
                              scaled.reshape(group_shape + (width,)).astype(jnp.float32)).astype(jnp.bfloat16)
        grad_in = jnp.sum(part_in.astype(jnp.float32), axis=0)
        grad_out = jnp.sum(part_out.astype(jnp.float32), axis=0)
        return (token_sum, gate_out), (grad_in, grad_out)

    initial = (jnp.zeros((TOKENS, tokens.shape[1]), jnp.float32), jnp.zeros((routes,), jnp.bfloat16))
    (token_sum, gate_out), (grad_weight_in, grad_weight_out) = lax.scan(
        one_expert, initial, (slot_table, weight_in, weight_out))
    grad_tokens = token_sum.astype(jnp.bfloat16)
    grad_gates = gate_out.reshape(TOKENS, 2)
    return grad_tokens, grad_gates, grad_weight_in, grad_weight_out
```

```python
import jax
import jax.numpy as jnp
from jax import lax
from jax.experimental import pallas as pl
from jax.experimental.pallas import tpu as pltpu
from jax.sharding import PartitionSpec as P

NX, NY, NZ = 4, 8, 8
SLOTS = 16
LANES = 128
SUB = 32
TICKS = 12
VMEM = pltpu.VMEM
F32, BF16 = jnp.float32, jnp.bfloat16
PLUS, MINUS = 0, 1
BLOCKS = ((0, 128), (128, 128), (256, 96), (352, 32))
FORWARD = {0: 4, 1: 5, 2: 6, 3: 7, 4: 8, 5: 9, 6: 10, 8: 11}
BACKWARD_DEP = {after: before for before, after in FORWARD.items()}


def dot(a, b, dims):
    return lax.dot_general(a, b, (dims, ((), ())), preferred_element_type=F32)


def places():
    dp, ex = lax.axis_index("dp"), lax.axis_index("expert")
    return lax.div(dp, 2), lax.rem(dp, 2), lax.div(ex, NX), lax.rem(ex, NX)


def wrap(i, n):
    return lax.rem(i + n, n)


def device(y, c, z, x):
    return (y * 2 + c, z * NX + x)


def remote(src, dst, send, recv, to):
    return pltpu.make_async_remote_copy(
        src_ref=src, dst_ref=dst, send_sem=send, recv_sem=recv, device_id=to, device_id_type=pl.DeviceIdType.MESH
    )


def greet(y, c, z, x):
    peers = [device(y, c, wrap(z + d, NZ), x) for d in (1, -1)]
    peers += [device(y, c, z, lax.rem(x + d, NX)) for d in (1, 2, 3)]
    peers += [device(wrap(y + d, NY), c, z, x) for d in (1, -1)]
    peers += [device(y, 1 - c, z, x)]
    barrier = pltpu.get_barrier_semaphore()
    for peer in peers:
        pl.semaphore_signal(barrier, inc=1, device_id=peer, device_id_type=pl.DeviceIdType.MESH)
    pl.semaphore_wait(barrier, len(peers))


def prepare_kernel(tok, grad, ids, gates, own, plus, minus, perm_plus, perm_minus):
    n, width = tok.shape
    z = lax.div(lax.axis_index("expert"), NX)
    lane = lax.broadcasted_iota(jnp.int32, (n, LANES), 1)
    row = lax.broadcasted_iota(jnp.int32, (n, LANES), 0)
    before = (lane < row).astype(BF16)
    id0, id1 = ids[:, 0:1], ids[:, 1:2]
    g0, g1 = gates[:, 0:1].astype(F32), gates[:, 1:2].astype(F32)

    def pick(table, at):
        return jnp.sum(jnp.where(lane == at, table, 0.0), axis=1, keepdims=True)

    hit = ((lane == id0) | (lane == id1)).astype(BF16)
    earlier = dot(before, hit, ((1,), (0,)))
    rank0, rank1 = pick(earlier, id0), pick(earlier, id1)
    p0, p1 = lax.shift_right_logical(id0, 2), lax.shift_right_logical(id1, 2)
    hit_plane = ((lane == p0) | (lane == p1)).astype(F32)
    earlier_plane = dot(before, hit_plane.astype(BF16), ((1,), (0,)))
    far = lax.rem(z + 4, NZ)
    in_far = pick(hit_plane, far)
    far_rank = pick(earlier_plane, far)
    low = jnp.where(far_rank < 32.0, 1.0, 0.0)

    def table(i0, i1):
        out = jnp.zeros((n, LANES), F32)
        for k, col in enumerate((i0, i1, rank0, rank1, g0, g1)):
            out = jnp.where(lane == k, col, out)
        return out.astype(BF16)

    f0, f1 = id0.astype(F32), id1.astype(F32)
    both = jnp.concatenate([tok[...], grad[...]], axis=1)
    own[:, : 2 * width] = both
    own[:, 2 * width :] = table(f0, f1)
    for out, perm, mine, at in ((plus, perm_plus, low, lax.rem(z + 3, NZ)), (minus, perm_minus, 1.0 - low, lax.rem(z + 5, NZ))):
        first = in_far * mine
        second = pick(hit_plane, at) * (1.0 - first)
        third = 1.0 - first - second
        sets = jnp.where(lane == 0, first, jnp.where(lane == 1, second, jnp.where(lane == 2, third, 0.0)))
        ahead = dot(before, sets.astype(BF16), ((1,), (0,)))
        totals = jnp.sum(sets, axis=0, keepdims=True)
        n0 = jnp.sum(jnp.where(lane == 0, totals, 0.0), axis=1, keepdims=True)
        n1 = jnp.sum(jnp.where(lane == 1, totals, 0.0), axis=1, keepdims=True)
        place = first * pick(ahead, 0) + second * (n0 + pick(ahead, 1)) + third * (n0 + n1 + pick(ahead, 2))
        order = (lane.astype(F32) == place).astype(BF16)
        perm[...] = order
        drop = 1.0 - mine
        i0 = jnp.where((p0 == far) & (drop > 0.5), 64.0, f0)
        i1 = jnp.where((p1 == far) & (drop > 0.5), 64.0, f1)
        order_t = order.T
        out[:, : 2 * width] = dot(order_t, both, ((1,), (0,))).astype(BF16)
        out[:, 2 * width :] = dot(order_t, table(i0, i1), ((1,), (0,))).astype(BF16)


def prepare(tok, grad, ids, gates):
    n, width = tok.shape
    rows = jax.ShapeDtypeStruct((n, 2 * width + LANES), BF16)
    perm = jax.ShapeDtypeStruct((n, n), BF16)
    return pl.pallas_call(
        prepare_kernel,
        out_shape=(rows, rows, rows, perm, perm),
        in_specs=[pl.BlockSpec(memory_space=VMEM)] * 4,
        out_specs=(pl.BlockSpec(memory_space=VMEM),) * 5,
        name="prepare",
    )(tok, grad, ids, gates)


def match_table(columns, z):
    n = columns.shape[0]
    lane = lax.broadcasted_iota(jnp.int32, (n, NX * SLOTS), 1)
    expert = (z * NX + lax.div(lane, SLOTS)).astype(F32)
    rank = lax.rem(lane, SLOTS).astype(F32)
    c = columns.astype(F32)
    hit = ((c[:, 0:1] == expert) & (c[:, 2:3] == rank)) | ((c[:, 1:2] == expert) & (c[:, 3:4] == rank))
    return jnp.where(hit, 1.0, 0.0).astype(BF16)


def dispatch_kernel(own, plus, minus, w_in, w_out, slots, full_in, full_out, m_own, m_dirs,
                    arrived, staged, z_send, z_recv, x_send, x_recv, y_send, y_recv, c_send, c_recv):
    y, c, z, x = places()
    width = own.shape[1]
    data = width - LANES
    greet(y, c, z, x)
    source = (plus, minus)
    step = (1, -1)

    def z_copy(d, tick, src):
        return remote(src, arrived.at[d, pl.ds(SUB * tick, SUB)], z_send.at[d, tick], z_recv.at[d, tick],
                      device(y, c, wrap(z + step[d], NZ), x))

    for tick in range(4):
        for d in (PLUS, MINUS):
            z_copy(d, tick, source[d].at[pl.ds(SUB * tick, SUB)]).start()

    def in_slot(yy, cc):
        return full_in.at[pl.ds(pl.multiple_of((yy * 2 + cc) * 128, 128), 128), :]

    def out_slot(yy, cc):
        return full_out.at[:, pl.ds(pl.multiple_of((yy * 2 + cc) * 128, 128), 128)]

    slot_of = (in_slot, out_slot)
    shard = (w_in, w_out)
    parts = {(d, h): (0, 1) for d in (0, 1) for h in (1, 2, 3)}
    parts[(0, 4)], parts[(1, 4)] = (0,), (1,)

    def y_copy(d, hop, part, src):
        origin = wrap(y - step[d] * (hop - 1) + NY, NY)
        return remote(src, slot_of[part](origin, c), y_send.at[d, hop - 1, part], y_recv.at[d, hop - 1, part],
                      device(wrap(y + step[d], NY), c, z, x))

    def c_copy(k, part, origin, src):
        return remote(src, slot_of[part](origin, c), c_send.at[k, part], c_recv.at[k, part], device(y, 1 - c, z, x))

    for part in (0, 1):
        for d in (0, 1):
            y_copy(d, 1, part, shard[part]).start()
        c_copy(0, part, y, shard[part]).start()
    in_slot(y, c)[...] = w_in[...]
    out_slot(y, c)[...] = w_out[...]

    def partner_index(d, hop):
        return 7 if hop == 4 else 3 * d + hop

    def y_step(hop):
        for d in (0, 1):
            origin = wrap(y - step[d] * hop + NY, NY)
            for part in parts[(d, hop)]:
                here = slot_of[part](origin, c)
                remote(here, here, y_send.at[d, hop - 1, part], y_recv.at[d, hop - 1, part],
                       device(wrap(y + step[d], NY), c, z, x)).wait_recv()
                if part in parts.get((d, hop + 1), ()):
                    y_copy(d, hop + 1, part, here).start()
                c_copy(partner_index(d, hop), part, origin, here).start()

    def x_copy(k, dx, origin_z):
        to = lax.rem(x + dx, NX)
        return remote(
            staged.at[k, pl.ds(pl.multiple_of(to * SLOTS, SLOTS), SLOTS)],
            slots.at[pl.ds(pl.multiple_of((origin_z * NX + x) * SLOTS, SLOTS), SLOTS)],
            x_send.at[k, dx - 1], x_recv.at[k, dx - 1], device(y, c, z, to))

    def send_selected(k, origin_z):
        for dx in (1, 3, 2):
            x_copy(k, dx, origin_z).start()
        mine = staged[k, pl.ds(pl.multiple_of(x * SLOTS, SLOTS), SLOTS), :]
        slots[pl.ds(pl.multiple_of((origin_z * NX + x) * SLOTS, SLOTS), SLOTS), :] = mine

    m0 = match_table(own[:, data:], z)
    m_own[...] = m0
    staged[0] = dot(m0, own[...], ((0,), (0,))).astype(BF16)
    send_selected(0, z)

    def origin_of(d, hop):
        return wrap(z - step[d] * hop + NZ, NZ)

    def select(d, hop):
        at, n = BLOCKS[hop - 1]
        m = match_table(arrived[d, at : at + n, data:], z)
        m_dirs[d, at : at + n] = m
        return dot(m, arrived[d, at : at + n, :], ((0,), (0,)))

    for tick in range(TICKS):
        for d in (PLUS, MINUS):
            here = arrived.at[d, pl.ds(SUB * tick, SUB)]
            z_copy(d, tick, here).wait_recv()
            if tick in FORWARD:
                z_copy(d, FORWARD[tick], here).start()
        if tick < 4:
            y_step(tick + 1)
        hop = {3: 1, 7: 2, 10: 3}.get(tick)
        if hop:
            for d in (PLUS, MINUS):
                k = 2 * hop - 1 + d
                staged[k] = select(d, hop).astype(BF16)
                send_selected(k, origin_of(d, hop))
    staged[7] = (select(PLUS, 4) + select(MINUS, 4)).astype(BF16)
    send_selected(7, origin_of(PLUS, 4))

    order = [(0, z)] + [(2 * h - 1 + d, origin_of(d, h)) for h in (1, 2, 3) for d in (0, 1)] + [(7, origin_of(0, 4))]
    for k, origin_z in order:
        for dx in (1, 2, 3):
            sender = lax.rem(x + NX - dx, NX)
            there = slots.at[pl.ds(pl.multiple_of((origin_z * NX + sender) * SLOTS, SLOTS), SLOTS)]
            remote(there, there, x_send.at[k, dx - 1], x_recv.at[k, dx - 1],
                   device(y, c, z, sender)).wait_recv()
            x_copy(k, dx, origin_z).wait_send()
    for k, origin, which in ([(0, y, (0, 1))]
                             + [(3 * d + h, wrap(y - step[d] * h + NY, NY), (0, 1)) for d in (0, 1) for h in (1, 2, 3)]
                             + [(7, wrap(y + 4, NY), (0, 1))]):
        for part in which:
            there = slot_of[part](origin, 1 - c)
            remote(there, there, c_send.at[k, part], c_recv.at[k, part], device(y, 1 - c, z, x)).wait_recv()
            src = shard[part] if k == 0 else slot_of[part](origin, c)
            c_copy(k, part, origin, src).wait_send()
    for (d, hop), which in parts.items():
        for part in which:
            origin = wrap(y - step[d] * (hop - 1) + NY, NY)
            src = shard[part] if hop == 1 else slot_of[part](origin, c)
            y_copy(d, hop, part, src).wait_send()
    back = {after: before for before, after in FORWARD.items()}
    for tick in range(TICKS):
        for d in (PLUS, MINUS):
            if tick < 4:
                src = source[d].at[pl.ds(SUB * tick, SUB)]
            else:
                src = arrived.at[d, pl.ds(SUB * back[tick], SUB)]
            z_copy(d, tick, src).wait_send()


def dispatch(own, plus, minus, w_in, w_out):
    width = own.shape[1]
    experts = NX * NZ
    hidden = w_in.shape[1]
    model = w_in.shape[0] * 2 * NY
    dma = pltpu.SemaphoreType.DMA
    return pl.pallas_call(
        dispatch_kernel,
        out_shape=(
            jax.ShapeDtypeStruct((experts * SLOTS, width), BF16),
            jax.ShapeDtypeStruct((model, hidden), BF16),
            jax.ShapeDtypeStruct((hidden, model), BF16),
            jax.ShapeDtypeStruct((own.shape[0], NX * SLOTS), BF16),
            jax.ShapeDtypeStruct((2, SUB * TICKS, NX * SLOTS), BF16),
        ),
        in_specs=[pl.BlockSpec(memory_space=VMEM)] * 5,
        out_specs=(pl.BlockSpec(memory_space=VMEM),) * 5,
        scratch_shapes=[
            VMEM((2, SUB * TICKS, width), BF16),
            VMEM((8, NX * SLOTS, width), BF16),
            dma((2, TICKS)), dma((2, TICKS)),
            dma((8, 3)), dma((8, 3)),
            dma((2, 4, 2)), dma((2, 4, 2)),
            dma((8, 2)), dma((8, 2)),
        ],
        compiler_params=pltpu.CompilerParams(collective_id=0, has_side_effects=True),
        name="dispatch",
    )(own, plus, minus, w_in, w_out)


def experts_kernel(slots, full_in, full_out, results, part_in, part_out, pre_grad, hidden_act, scaled):
    rows, width = slots.shape
    model, hidden = full_in.shape
    ex = lax.axis_index("expert").astype(F32)
    chunk = 128

    def forward(i, _):
        at = pl.ds(pl.multiple_of(i * chunk, chunk), chunk)
        columns = slots[at, 2 * model :].astype(F32)
        first = columns[:, 0:1] == ex
        gate = jnp.where(first, columns[:, 4:5], columns[:, 5:6])
        grad = slots[at, model : 2 * model]
        preact = dot(slots[at, :model], full_in[...], ((1,), (0,)))
        back = dot(grad, full_out[...], ((1,), (1,)))
        s = jax.nn.sigmoid(preact)
        act = (preact * s).astype(BF16)
        hidden_act[at, :] = act
        gate_grad = jnp.sum(act.astype(F32) * back, axis=1, keepdims=True)
        pre = (gate * back * (s * (1.0 + preact * (1.0 - s)))).astype(BF16)
        pre_grad[at, :] = pre
        scaled[at, :] = (gate * grad.astype(F32)).astype(BF16)
        results[at, :model] = dot(pre, full_in[...], ((1,), (1,))).astype(BF16)
        lane = lax.broadcasted_iota(jnp.int32, (chunk, LANES), 1)
        column = jnp.where(first, 0, 1)
        results[at, model:] = jnp.where(lane == column, gate_grad, 0.0).astype(BF16)
        return 0

    lax.fori_loop(0, rows // chunk, forward, 0)

    for k in range(model // 512):
        term = dot(slots[:, 512 * k : 512 * (k + 1)], pre_grad[...], ((0,), (0,))).astype(BF16)
        for j in range(4):
            dp = 4 * k + j
            part_in[dp % 2, dp // 2] = term[128 * j : 128 * (j + 1), :]
        term = dot(hidden_act[...], scaled[:, 512 * k : 512 * (k + 1)], ((0,), (0,))).astype(BF16)
        for j in range(4):
            dp = 4 * k + j
            part_out[dp % 2, dp // 2] = term[:, 128 * j : 128 * (j + 1)]


def run_experts(slots, full_in, full_out):
    rows = slots.shape[0]
    model, hidden = full_in.shape
    share = model // (2 * NY)
    return pl.pallas_call(
        experts_kernel,
        out_shape=(
            jax.ShapeDtypeStruct((rows, model + LANES), BF16),
            jax.ShapeDtypeStruct((2, NY, share, hidden), BF16),
            jax.ShapeDtypeStruct((2, NY, hidden, share), BF16),
        ),
        in_specs=[pl.BlockSpec(memory_space=VMEM)] * 3,
        out_specs=(pl.BlockSpec(memory_space=VMEM),) * 3,
        scratch_shapes=[VMEM((rows, hidden), BF16), VMEM((rows, hidden), BF16), VMEM((rows, model), BF16)],
        name="experts",
    )(slots, full_in, full_out)


def collect_kernel(results, part_in, part_out, m_own, m_dirs, perm_plus, perm_minus,
                   grad_tokens, grad_gates, grad_in, grad_out,
                   gathered, outgoing, arrived, partner_in, partner_out, sum_in, sum_out, got_in, got_out,
                   z_send, z_recv, x_send, x_recv, y_send, y_recv, c_send, c_recv):
    y, c, z, x = places()
    model = grad_tokens.shape[1]
    greet(y, c, z, x)
    step = (1, -1)
    partner = device(y, 1 - c, z, x)
    mine_t, partner_t, sum_t, got_t = (part_in, part_out), (partner_in, partner_out), (sum_in, sum_out), (got_in, got_out)

    def origin_of(d, hop):
        return wrap(z - step[d] * hop + NZ, NZ)

    planes = [(7, origin_of(0, 4))] + [(2 * h - 1 + d, origin_of(d, h)) for h in (3, 2, 1) for d in (0, 1)] + [(0, z)]

    def x_copy(k, dx, origin_z):
        to = lax.rem(x + dx, NX)
        return remote(
            results.at[pl.ds(pl.multiple_of((origin_z * NX + to) * SLOTS, SLOTS), SLOTS)],
            gathered.at[k, pl.ds(pl.multiple_of(x * SLOTS, SLOTS), SLOTS)],
            x_send.at[k, dx - 1], x_recv.at[k, dx - 1], device(y, c, z, to))

    for k, origin_z in planes:
        for dx in (1, 3, 2):
            x_copy(k, dx, origin_z).start()

    def c_copy(part):
        return remote(mine_t[part].at[1 - c], partner_t[part], c_send.at[part], c_recv.at[part], partner)

    for part in (0, 1):
        c_copy(part).start()
    for k, origin_z in planes:
        at = pl.ds(pl.multiple_of(x * SLOTS, SLOTS), SLOTS)
        gathered[k, at, :] = results[pl.ds(pl.multiple_of((origin_z * NX + x) * SLOTS, SLOTS), SLOTS), :]

    def x_wait(k):
        for dx in (1, 2, 3):
            sender = lax.rem(x + NX - dx, NX)
            there = gathered.at[k, pl.ds(pl.multiple_of(sender * SLOTS, SLOTS), SLOTS)]
            remote(there, there, x_send.at[k, dx - 1], x_recv.at[k, dx - 1], device(y, c, z, sender)).wait_recv()

    def z_copy(d, tick):
        at = pl.ds(SUB * tick, SUB)
        return remote(outgoing.at[d, at], arrived.at[d, at], z_send.at[d, tick], z_recv.at[d, tick],
                      device(y, c, wrap(z - step[d], NZ), x))

    def z_step(tick, hop):
        for d in (PLUS, MINUS):
            k = 7 if hop == 4 else 2 * hop - 1 + d
            rows = dot(m_dirs[d, SUB * tick : SUB * (tick + 1), :], gathered[k], ((1,), (0,)))
            later = FORWARD.get(tick)
            if later is not None:
                z_copy(d, later).wait_recv()
                rows = rows + arrived[d, SUB * later : SUB * (later + 1), :].astype(F32)
            outgoing[d, SUB * tick : SUB * (tick + 1), :] = rows.astype(BF16)
            z_copy(d, tick).start()

    y_parts = {(d, h): (0, 1) for d in (0, 1) for h in (1, 2, 3)}
    y_parts[(0, 4)], y_parts[(1, 4)] = (0,), (1,)

    def y_copy(d, hop, part):
        return remote(sum_t[part].at[d, hop - 1], got_t[part].at[d, hop - 1], y_send.at[d, hop - 1, part],
                      y_recv.at[d, hop - 1, part], device(wrap(y - step[d], NY), c, z, x))

    def y_step(hop):
        for d in (0, 1):
            target = wrap(y - step[d] * hop + NY, NY)
            for part in y_parts[(d, hop)]:
                total = mine_t[part][c, target].astype(F32) + partner_t[part][target].astype(F32)
                if part in y_parts.get((d, hop + 1), ()):
                    y_copy(d, hop + 1, part).wait_recv()
                    total = total + got_t[part][d, hop].astype(F32)
                sum_t[part][d, hop - 1] = total.astype(BF16)
                y_copy(d, hop, part).start()

    x_wait(7)
    z_step(11, 4)
    for part in (0, 1):
        c_copy(part).wait_recv()
    y_step(4)
    x_wait(5)
    x_wait(6)
    z_step(9, 3)
    z_step(10, 3)
    z_step(8, 3)
    y_step(3)
    x_wait(3)
    x_wait(4)
    z_step(7, 2)
    z_step(5, 2)
    z_step(6, 2)
    z_step(4, 2)
    y_step(2)
    x_wait(1)
    x_wait(2)
    z_step(1, 1)
    z_step(2, 1)
    y_step(1)
    z_step(0, 1)
    z_step(3, 1)
    x_wait(0)
    total = dot(m_own[...], gathered[0], ((1,), (0,)))
    for part, out in ((0, grad_in), (1, grad_out)):
        acc = mine_t[part][c, y].astype(F32) + partner_t[part][y].astype(F32)
        for d in (0, 1):
            y_copy(d, 1, part).wait_recv()
            acc = acc + got_t[part][d, 0].astype(F32)
        out[...] = acc
    for tick in (1, 2, 0, 3):
        for d in (PLUS, MINUS):
            z_copy(d, tick).wait_recv()
    for d, perm in ((PLUS, perm_plus), (MINUS, perm_minus)):
        total = total + dot(perm[...], arrived[d, 0:128, :], ((1,), (0,)))
    grad_tokens[...] = total[:, :model].astype(BF16)
    grad_gates[...] = total[:, model : model + 2].astype(BF16)

    for k, origin_z in planes:
        for dx in (1, 2, 3):
            x_copy(k, dx, origin_z).wait_send()
    for part in (0, 1):
        c_copy(part).wait_send()
    for (d, hop), which in y_parts.items():
        for part in which:
            y_copy(d, hop, part).wait_send()
    for tick in range(TICKS):
        for d in (PLUS, MINUS):
            z_copy(d, tick).wait_send()


def collect(results, part_in, part_out, m_own, m_dirs, perm_plus, perm_minus):
    width = results.shape[1]
    model = width - LANES
    n = m_own.shape[0]
    _, _, share, hidden = part_in.shape
    dma = pltpu.SemaphoreType.DMA
    shard_in, shard_out = (share, hidden), (hidden, share)
    return pl.pallas_call(
        collect_kernel,
        out_shape=(
            jax.ShapeDtypeStruct((n, model), BF16),
            jax.ShapeDtypeStruct((n, 2), BF16),
            jax.ShapeDtypeStruct(shard_in, F32),
            jax.ShapeDtypeStruct(shard_out, F32),
        ),
        in_specs=[pl.BlockSpec(memory_space=VMEM)] * 7,
        out_specs=(pl.BlockSpec(memory_space=VMEM),) * 4,
        scratch_shapes=[
            VMEM((8, NX * SLOTS, width), BF16),
            VMEM((2, SUB * TICKS, width), BF16),
            VMEM((2, SUB * TICKS, width), BF16),
            VMEM((NY,) + shard_in, BF16), VMEM((NY,) + shard_out, BF16),
            VMEM((2, 4) + shard_in, BF16), VMEM((2, 4) + shard_out, BF16),
            VMEM((2, 4) + shard_in, BF16), VMEM((2, 4) + shard_out, BF16),
            dma((2, TICKS)), dma((2, TICKS)),
            dma((8, 3)), dma((8, 3)),
            dma((2, 4, 2)), dma((2, 4, 2)),
            dma((2,)), dma((2,)),
        ],
        compiler_params=pltpu.CompilerParams(collective_id=1, has_side_effects=True),
        name="collect",
    )(results, part_in, part_out, m_own, m_dirs, perm_plus, perm_minus)


def on_device(tokens, out_grad, route_ids, route_gates, weight_in, weight_out):
    own, plus, minus, perm_plus, perm_minus = prepare(tokens, out_grad, route_ids, route_gates)
    slots, full_in, full_out, m_own, m_dirs = dispatch(own, plus, minus, weight_in[0], weight_out[0])
    results, part_in, part_out = run_experts(slots, full_in, full_out)
    grad_tokens, grad_gates, grad_in, grad_out = collect(
        results, part_in, part_out, m_own, m_dirs, perm_plus, perm_minus
    )
    return grad_tokens, grad_gates, grad_in[None], grad_out[None]


def solution(mesh):
    rows = P(("dp", "expert"), None)
    return jax.shard_map(
        on_device,
        mesh=mesh,
        in_specs=(rows, rows, rows, rows, P("expert", "dp", None), P("expert", None, "dp")),
        out_specs=(rows, rows, P("expert", "dp", None), P("expert", None, "dp")),
        check_vma=False,
    )
```

```python
import jax
import jax.numpy as jnp
from jax import lax
from jax.experimental import pallas as pl
from jax.experimental.pallas import tpu as pltpu
from jax.sharding import PartitionSpec as P

NX, NY, NZ = 4, 8, 8
SLOTS = 16
LANES = 128
SUB = 32
TICKS = 12
VMEM = pltpu.VMEM
F32, BF16 = jnp.float32, jnp.bfloat16
PLUS, MINUS = 0, 1
BLOCKS = ((0, 128), (128, 128), (256, 96), (352, 32))
FORWARD = {0: 4, 1: 5, 2: 6, 3: 7, 4: 8, 5: 9, 6: 10, 8: 11}
BACKWARD_DEP = {after: before for before, after in FORWARD.items()}


def dot(a, b, dims):
    return lax.dot_general(a, b, (dims, ((), ())), preferred_element_type=F32)


def places():
    dp, ex = lax.axis_index("dp"), lax.axis_index("expert")
    return lax.div(dp, 2), lax.rem(dp, 2), lax.div(ex, NX), lax.rem(ex, NX)


def wrap(i, n):
    return lax.rem(i + n, n)


def device(y, c, z, x):
    return (y * 2 + c, z * NX + x)


def remote(src, dst, send, recv, to):
    return pltpu.make_async_remote_copy(
        src_ref=src, dst_ref=dst, send_sem=send, recv_sem=recv, device_id=to, device_id_type=pl.DeviceIdType.MESH
    )


def via(k):
    return NX - 1 if k % 2 else 1


def greet(y, c, z, x):
    peers = [device(y, c, wrap(z + d, NZ), x) for d in (1, -1)]
    peers += [device(y, c, z, lax.rem(x + d, NX)) for d in (1, 2, 3)]
    peers += [device(wrap(y + d, NY), c, z, x) for d in (1, -1)]
    peers += [device(y, 1 - c, z, x)]
    barrier = pltpu.get_barrier_semaphore()
    for peer in peers:
        pl.semaphore_signal(barrier, inc=1, device_id=peer, device_id_type=pl.DeviceIdType.MESH)
    pl.semaphore_wait(barrier, len(peers))


def prepare_kernel(tok, grad, ids, gates, own, plus, minus, perm_plus, perm_minus):
    n, width = tok.shape
    z = lax.div(lax.axis_index("expert"), NX)
    lane = lax.broadcasted_iota(jnp.int32, (n, LANES), 1)
    row = lax.broadcasted_iota(jnp.int32, (n, LANES), 0)
    before = (lane < row).astype(BF16)
    columns = jnp.concatenate([ids[...].astype(F32), gates[...].astype(F32), jnp.zeros((4, n), F32)], axis=0).T
    f0, f1, g0, g1 = (columns[:, k : k + 1] for k in range(4))
    id0, id1 = f0.astype(jnp.int32), f1.astype(jnp.int32)

    def pick(table, at):
        return jnp.sum(jnp.where(lane == at, table, 0.0), axis=1, keepdims=True)

    hit = ((lane == id0) | (lane == id1)).astype(BF16)
    earlier = dot(before, hit, ((1,), (0,)))
    rank0, rank1 = pick(earlier, id0), pick(earlier, id1)
    p0, p1 = lax.shift_right_logical(id0, 2), lax.shift_right_logical(id1, 2)
    hit_plane = ((lane == p0) | (lane == p1)).astype(F32)
    earlier_plane = dot(before, hit_plane.astype(BF16), ((1,), (0,)))
    far = lax.rem(z + 4, NZ)
    in_far = pick(hit_plane, far)
    far_rank = pick(earlier_plane, far)
    low = jnp.where(far_rank < 32.0, 1.0, 0.0)

    def table(i0, i1):
        out = jnp.zeros((n, LANES), F32)
        for k, col in enumerate((i0, i1, rank0, rank1, g0, g1)):
            out = jnp.where(lane == k, col, out)
        return out.astype(BF16)

    both = jnp.concatenate([tok[...], grad[...]], axis=1)
    own[:, : 2 * width] = both
    own[:, 2 * width :] = table(f0, f1)
    for out, perm, mine, at in ((plus, perm_plus, low, lax.rem(z + 3, NZ)), (minus, perm_minus, 1.0 - low, lax.rem(z + 5, NZ))):
        first = in_far * mine
        second = pick(hit_plane, at) * (1.0 - first)
        third = 1.0 - first - second
        sets = jnp.where(lane == 0, first, jnp.where(lane == 1, second, jnp.where(lane == 2, third, 0.0)))
        ahead = dot(before, sets.astype(BF16), ((1,), (0,)))
        totals = jnp.sum(sets, axis=0, keepdims=True)
        n0 = jnp.sum(jnp.where(lane == 0, totals, 0.0), axis=1, keepdims=True)
        n1 = jnp.sum(jnp.where(lane == 1, totals, 0.0), axis=1, keepdims=True)
        place = first * pick(ahead, 0) + second * (n0 + pick(ahead, 1)) + third * (n0 + n1 + pick(ahead, 2))
        order = (lane.astype(F32) == place).astype(BF16)
        perm[...] = order
        drop = 1.0 - mine
        i0 = jnp.where((p0 == far) & (drop > 0.5), 64.0, f0)
        i1 = jnp.where((p1 == far) & (drop > 0.5), 64.0, f1)
        order_t = order.T
        out[:, : 2 * width] = dot(order_t, both, ((1,), (0,))).astype(BF16)
        out[:, 2 * width :] = dot(order_t, table(i0, i1), ((1,), (0,))).astype(BF16)


def prepare(tok, grad, ids, gates):
    n, width = tok.shape
    rows = jax.ShapeDtypeStruct((n, 2 * width + LANES), BF16)
    perm = jax.ShapeDtypeStruct((n, n), BF16)
    return pl.pallas_call(
        prepare_kernel,
        out_shape=(rows, rows, rows, perm, perm),
        in_specs=[pl.BlockSpec(memory_space=VMEM)] * 4,
        out_specs=(pl.BlockSpec(memory_space=VMEM),) * 5,
        name="prepare",
    )(tok, grad, ids, gates)


def match_table(columns, z):
    n = columns.shape[0]
    lane = lax.broadcasted_iota(jnp.int32, (n, NX * SLOTS), 1)
    expert = (z * NX + lax.div(lane, SLOTS)).astype(F32)
    rank = lax.rem(lane, SLOTS).astype(F32)
    c = columns.astype(F32)
    hit = ((c[:, 0:1] == expert) & (c[:, 2:3] == rank)) | ((c[:, 1:2] == expert) & (c[:, 3:4] == rank))
    return jnp.where(hit, 1.0, 0.0).astype(BF16)


def dispatch_kernel(own, plus, minus, w_in, w_out, slots, full_in, full_out, m_own, m_dirs,
                    arrived, staged, passing, z_send, z_recv, x_send, x_recv, p_send, p_recv,
                    y_send, y_recv, c_send, c_recv):
    y, c, z, x = places()
    width = own.shape[1]
    data = width - LANES
    greet(y, c, z, x)
    source = (plus, minus)
    step = (1, -1)

    def z_copy(d, tick, src):
        return remote(src, arrived.at[d, pl.ds(SUB * tick, SUB)], z_send.at[d, tick], z_recv.at[d, tick],
                      device(y, c, wrap(z + step[d], NZ), x))

    for tick in range(4):
        for d in (PLUS, MINUS):
            z_copy(d, tick, source[d].at[pl.ds(SUB * tick, SUB)]).start()

    def in_slot(yy, cc):
        return full_in.at[pl.ds(pl.multiple_of((yy * 2 + cc) * 128, 128), 128), :]

    def out_slot(yy, cc):
        return full_out.at[:, pl.ds(pl.multiple_of((yy * 2 + cc) * 128, 128), 128)]

    slot_of = (in_slot, out_slot)
    shard = (w_in, w_out)
    parts = {(d, h): (0, 1) for d in (0, 1) for h in (1, 2, 3)}
    parts[(0, 4)], parts[(1, 4)] = (0,), (1,)

    def y_copy(d, hop, part, src):
        origin = wrap(y - step[d] * (hop - 1) + NY, NY)
        return remote(src, slot_of[part](origin, c), y_send.at[d, hop - 1, part], y_recv.at[d, hop - 1, part],
                      device(wrap(y + step[d], NY), c, z, x))

    def c_copy(k, part, origin, src):
        return remote(src, slot_of[part](origin, c), c_send.at[k, part], c_recv.at[k, part], device(y, 1 - c, z, x))

    for part in (0, 1):
        for d in (0, 1):
            y_copy(d, 1, part, shard[part]).start()
        c_copy(0, part, y, shard[part]).start()
    in_slot(y, c)[...] = w_in[...]
    out_slot(y, c)[...] = w_out[...]

    def partner_index(d, hop):
        return 7 if hop == 4 else 3 * d + hop

    def y_step(hop):
        for d in (0, 1):
            origin = wrap(y - step[d] * hop + NY, NY)
            for part in parts[(d, hop)]:
                here = slot_of[part](origin, c)
                remote(here, here, y_send.at[d, hop - 1, part], y_recv.at[d, hop - 1, part],
                       device(wrap(y + step[d], NY), c, z, x)).wait_recv()
                if part in parts.get((d, hop + 1), ()):
                    y_copy(d, hop + 1, part, here).start()
                c_copy(partner_index(d, hop), part, origin, here).start()

    def slot_rows(origin_z, origin_x):
        return slots.at[pl.ds(pl.multiple_of((origin_z * NX + origin_x) * SLOTS, SLOTS), SLOTS)]

    def x_copy(k, dx, origin_z):
        to = lax.rem(x + dx, NX)
        src = staged.at[k, pl.ds(pl.multiple_of(to * SLOTS, SLOTS), SLOTS)]
        if dx == 2:
            return remote(src, passing.at[k], x_send.at[k, 1], x_recv.at[k, 1],
                          device(y, c, z, lax.rem(x + via(k), NX)))
        return remote(src, slot_rows(origin_z, x), x_send.at[k, dx - 1], x_recv.at[k, dx - 1], device(y, c, z, to))

    def pass_copy(k, origin_z):
        return remote(passing.at[k], slot_rows(origin_z, lax.rem(x + NX - via(k), NX)), p_send.at[k], p_recv.at[k],
                      device(y, c, z, lax.rem(x + via(k), NX)))

    def pass_on(k, origin_z):
        remote(passing.at[k], passing.at[k], x_send.at[k, 1], x_recv.at[k, 1],
               device(y, c, z, lax.rem(x + NX - via(k), NX))).wait_recv()
        pass_copy(k, origin_z).start()

    def send_selected(k, origin_z):
        for dx in (2, 1, 3):
            x_copy(k, dx, origin_z).start()
        mine = staged[k, pl.ds(pl.multiple_of(x * SLOTS, SLOTS), SLOTS), :]
        slots[pl.ds(pl.multiple_of((origin_z * NX + x) * SLOTS, SLOTS), SLOTS), :] = mine

    m0 = match_table(own[:, data:], z)
    m_own[...] = m0
    staged[0] = dot(m0, own[...], ((0,), (0,))).astype(BF16)
    send_selected(0, z)

    def origin_of(d, hop):
        return wrap(z - step[d] * hop + NZ, NZ)

    def select(d, hop):
        at, n = BLOCKS[hop - 1]
        m = match_table(arrived[d, at : at + n, data:], z)
        m_dirs[d, at : at + n] = m
        return dot(m, arrived[d, at : at + n, :], ((0,), (0,)))

    for tick in range(TICKS):
        for d in (PLUS, MINUS):
            here = arrived.at[d, pl.ds(SUB * tick, SUB)]
            z_copy(d, tick, here).wait_recv()
            if tick in FORWARD:
                z_copy(d, FORWARD[tick], here).start()
        if tick < 4:
            y_step(tick + 1)
        if tick == 1:
            pass_on(0, z)
        if tick in (5, 9):
            for d in (PLUS, MINUS):
                hop = 1 if tick == 5 else 2
                pass_on(2 * hop - 1 + d, origin_of(d, hop))
        hop = {3: 1, 7: 2, 10: 3}.get(tick)
        if hop:
            for d in (PLUS, MINUS):
                k = 2 * hop - 1 + d
                staged[k] = select(d, hop).astype(BF16)
                send_selected(k, origin_of(d, hop))
    staged[7] = (select(PLUS, 4) + select(MINUS, 4)).astype(BF16)
    send_selected(7, origin_of(PLUS, 4))
    for d in (PLUS, MINUS):
        pass_on(5 + d, origin_of(d, 3))
    pass_on(7, origin_of(PLUS, 4))

    order = [(0, z)] + [(2 * h - 1 + d, origin_of(d, h)) for h in (1, 2, 3) for d in (0, 1)] + [(7, origin_of(0, 4))]
    for k, origin_z in order:
        for dx in (1, 3):
            sender = lax.rem(x + NX - dx, NX)
            there = slot_rows(origin_z, sender)
            remote(there, there, x_send.at[k, dx - 1], x_recv.at[k, dx - 1],
                   device(y, c, z, sender)).wait_recv()
        there = slot_rows(origin_z, lax.rem(x + 2, NX))
        remote(there, there, p_send.at[k], p_recv.at[k], device(y, c, z, lax.rem(x + NX - via(k), NX))).wait_recv()
        for dx in (1, 2, 3):
            x_copy(k, dx, origin_z).wait_send()
        pass_copy(k, origin_z).wait_send()
    for k, origin, which in ([(0, y, (0, 1))]
                             + [(3 * d + h, wrap(y - step[d] * h + NY, NY), (0, 1)) for d in (0, 1) for h in (1, 2, 3)]
                             + [(7, wrap(y + 4, NY), (0, 1))]):
        for part in which:
            there = slot_of[part](origin, 1 - c)
            remote(there, there, c_send.at[k, part], c_recv.at[k, part], device(y, 1 - c, z, x)).wait_recv()
            src = shard[part] if k == 0 else slot_of[part](origin, c)
            c_copy(k, part, origin, src).wait_send()
    for (d, hop), which in parts.items():
        for part in which:
            origin = wrap(y - step[d] * (hop - 1) + NY, NY)
            src = shard[part] if hop == 1 else slot_of[part](origin, c)
            y_copy(d, hop, part, src).wait_send()
    back = {after: before for before, after in FORWARD.items()}
    for tick in range(TICKS):
        for d in (PLUS, MINUS):
            if tick < 4:
                src = source[d].at[pl.ds(SUB * tick, SUB)]
            else:
                src = arrived.at[d, pl.ds(SUB * back[tick], SUB)]
            z_copy(d, tick, src).wait_send()


def dispatch(own, plus, minus, w_in, w_out):
    width = own.shape[1]
    experts = NX * NZ
    hidden = w_in.shape[1]
    model = w_in.shape[0] * 2 * NY
    dma = pltpu.SemaphoreType.DMA
    return pl.pallas_call(
        dispatch_kernel,
        out_shape=(
            jax.ShapeDtypeStruct((experts * SLOTS, width), BF16),
            jax.ShapeDtypeStruct((model, hidden), BF16),
            jax.ShapeDtypeStruct((hidden, model), BF16),
            jax.ShapeDtypeStruct((own.shape[0], NX * SLOTS), BF16),
            jax.ShapeDtypeStruct((2, SUB * TICKS, NX * SLOTS), BF16),
        ),
        in_specs=[pl.BlockSpec(memory_space=VMEM)] * 5,
        out_specs=(pl.BlockSpec(memory_space=VMEM),) * 5,
        scratch_shapes=[
            VMEM((2, SUB * TICKS, width), BF16),
            VMEM((8, NX * SLOTS, width), BF16),
            VMEM((8, SLOTS, width), BF16),
            dma((2, TICKS)), dma((2, TICKS)),
            dma((8, 3)), dma((8, 3)),
            dma((8,)), dma((8,)),
            dma((2, 4, 2)), dma((2, 4, 2)),
            dma((8, 2)), dma((8, 2)),
        ],
        compiler_params=pltpu.CompilerParams(collective_id=0, has_side_effects=True),
        name="dispatch",
    )(own, plus, minus, w_in, w_out)


def experts_kernel(slots, full_in, full_out, results, part_in, part_out, pre_grad, hidden_act, scaled):
    rows, width = slots.shape
    model, hidden = full_in.shape
    ex = lax.axis_index("expert").astype(F32)
    chunk = 128

    def forward(i, _):
        at = pl.ds(pl.multiple_of(i * chunk, chunk), chunk)
        columns = slots[at, 2 * model :].astype(F32)
        first = columns[:, 0:1] == ex
        gate = jnp.where(first, columns[:, 4:5], columns[:, 5:6])
        grad = slots[at, model : 2 * model]
        preact = dot(slots[at, :model], full_in[...], ((1,), (0,)))
        back = dot(grad, full_out[...], ((1,), (1,)))
        s = jax.nn.sigmoid(preact)
        act = (preact * s).astype(BF16)
        hidden_act[at, :] = act
        gate_grad = jnp.sum(act.astype(F32) * back, axis=1, keepdims=True)
        pre = (gate * back * (s * (1.0 + preact * (1.0 - s)))).astype(BF16)
        pre_grad[at, :] = pre
        scaled[at, :] = (gate * grad.astype(F32)).astype(BF16)
        results[at, :model] = dot(pre, full_in[...], ((1,), (1,))).astype(BF16)
        lane = lax.broadcasted_iota(jnp.int32, (chunk, LANES), 1)
        column = jnp.where(first, 0, 1)
        results[at, model:] = jnp.where(lane == column, gate_grad, 0.0).astype(BF16)
        return 0

    lax.fori_loop(0, rows // chunk, forward, 0)

    for k in range(model // 512):
        term = dot(slots[:, 512 * k : 512 * (k + 1)], pre_grad[...], ((0,), (0,))).astype(BF16)
        for j in range(4):
            dp = 4 * k + j
            part_in[dp % 2, dp // 2] = term[128 * j : 128 * (j + 1), :]
        term = dot(hidden_act[...], scaled[:, 512 * k : 512 * (k + 1)], ((0,), (0,))).astype(BF16)
        for j in range(4):
            dp = 4 * k + j
            part_out[dp % 2, dp // 2] = term[:, 128 * j : 128 * (j + 1)]


def run_experts(slots, full_in, full_out):
    rows = slots.shape[0]
    model, hidden = full_in.shape
    share = model // (2 * NY)
    return pl.pallas_call(
        experts_kernel,
        out_shape=(
            jax.ShapeDtypeStruct((rows, model + LANES), BF16),
            jax.ShapeDtypeStruct((2, NY, share, hidden), BF16),
            jax.ShapeDtypeStruct((2, NY, hidden, share), BF16),
        ),
        in_specs=[pl.BlockSpec(memory_space=VMEM)] * 3,
        out_specs=(pl.BlockSpec(memory_space=VMEM),) * 3,
        scratch_shapes=[VMEM((rows, hidden), BF16), VMEM((rows, hidden), BF16), VMEM((rows, model), BF16)],
        name="experts",
    )(slots, full_in, full_out)


def collect_kernel(results, part_in, part_out, m_own, m_dirs,
                   back, grad_in, grad_out,
                   gathered, passing, outgoing, arrived, partner_in, partner_out, sum_in, sum_out, got_in, got_out,
                   z_send, z_recv, x_send, x_recv, p_send, p_recv, y_send, y_recv, c_send, c_recv):
    y, c, z, x = places()
    greet(y, c, z, x)
    step = (1, -1)
    partner = device(y, 1 - c, z, x)
    mine_t, partner_t, sum_t, got_t = (part_in, part_out), (partner_in, partner_out), (sum_in, sum_out), (got_in, got_out)

    def origin_of(d, hop):
        return wrap(z - step[d] * hop + NZ, NZ)

    plane_of = {7: origin_of(0, 4), 0: z}
    for h in (1, 2, 3):
        for d in (0, 1):
            plane_of[2 * h - 1 + d] = origin_of(d, h)

    def gathered_rows(k, origin_x):
        return gathered.at[k, pl.ds(pl.multiple_of(origin_x * SLOTS, SLOTS), SLOTS)]

    def x_copy(k, dx):
        to = lax.rem(x + dx, NX)
        src = results.at[pl.ds(pl.multiple_of((plane_of[k] * NX + to) * SLOTS, SLOTS), SLOTS)]
        if dx == 2:
            return remote(src, passing.at[k], x_send.at[k, 1], x_recv.at[k, 1],
                          device(y, c, z, lax.rem(x + via(k), NX)))
        return remote(src, gathered_rows(k, x), x_send.at[k, dx - 1], x_recv.at[k, dx - 1], device(y, c, z, to))

    def pass_copy(k):
        return remote(passing.at[k], gathered_rows(k, lax.rem(x + NX - via(k), NX)), p_send.at[k], p_recv.at[k],
                      device(y, c, z, lax.rem(x + via(k), NX)))

    def x_start(*ks):
        for k in ks:
            for dx in (2, 1, 3):
                x_copy(k, dx).start()
            at = pl.ds(pl.multiple_of(x * SLOTS, SLOTS), SLOTS)
            gathered[k, at, :] = results[pl.ds(pl.multiple_of((plane_of[k] * NX + x) * SLOTS, SLOTS), SLOTS), :]

    def pass_on(*ks):
        for k in ks:
            remote(passing.at[k], passing.at[k], x_send.at[k, 1], x_recv.at[k, 1],
                   device(y, c, z, lax.rem(x + NX - via(k), NX))).wait_recv()
            pass_copy(k).start()

    def c_copy(part):
        return remote(mine_t[part].at[1 - c], partner_t[part], c_send.at[part], c_recv.at[part], partner)

    def x_wait(*ks):
        for k in ks:
            for dx in (1, 3):
                sender = lax.rem(x + NX - dx, NX)
                there = gathered_rows(k, sender)
                remote(there, there, x_send.at[k, dx - 1], x_recv.at[k, dx - 1], device(y, c, z, sender)).wait_recv()
            there = gathered_rows(k, lax.rem(x + 2, NX))
            remote(there, there, p_send.at[k], p_recv.at[k],
                   device(y, c, z, lax.rem(x + NX - via(k), NX))).wait_recv()

    def z_copy(d, tick):
        at = pl.ds(SUB * tick, SUB)
        dst = back.at[d, at] if tick < 4 else arrived.at[d, at]
        return remote(outgoing.at[d, at], dst, z_send.at[d, tick], z_recv.at[d, tick],
                      device(y, c, wrap(z - step[d], NZ), x))

    def z_step(tick, hop):
        for d in (PLUS, MINUS):
            k = 7 if hop == 4 else 2 * hop - 1 + d
            rows = dot(m_dirs[d, SUB * tick : SUB * (tick + 1), :], gathered[k], ((1,), (0,)))
            later = FORWARD.get(tick)
            if later is not None:
                z_copy(d, later).wait_recv()
                rows = rows + arrived[d, SUB * later : SUB * (later + 1), :].astype(F32)
            outgoing[d, SUB * tick : SUB * (tick + 1), :] = rows.astype(BF16)
            z_copy(d, tick).start()

    y_parts = {(d, h): (0, 1) for d in (0, 1) for h in (1, 2, 3)}
    y_parts[(0, 4)], y_parts[(1, 4)] = (0,), (1,)

    def y_copy(d, hop, part):
        return remote(sum_t[part].at[d, hop - 1], got_t[part].at[d, hop - 1], y_send.at[d, hop - 1, part],
                      y_recv.at[d, hop - 1, part], device(wrap(y - step[d], NY), c, z, x))

    def y_step(hop):
        for d in (0, 1):
            target = wrap(y - step[d] * hop + NY, NY)
            for part in y_parts[(d, hop)]:
                total = mine_t[part][c, target].astype(F32) + partner_t[part][target].astype(F32)
                if part in y_parts.get((d, hop + 1), ()):
                    y_copy(d, hop + 1, part).wait_recv()
                    total = total + got_t[part][d, hop].astype(F32)
                sum_t[part][d, hop - 1] = total.astype(BF16)
                y_copy(d, hop, part).start()

    x_start(7, 5)
    for part in (0, 1):
        c_copy(part).start()
    pass_on(7)
    x_start(6, 3)
    x_wait(7)
    z_step(11, 4)
    pass_on(5, 6)
    x_start(4, 1)
    for part in (0, 1):
        c_copy(part).wait_recv()
    y_step(4)
    x_wait(5, 6)
    z_step(9, 3)
    z_step(10, 3)
    pass_on(3, 4)
    x_start(2, 0)
    z_step(8, 3)
    y_step(3)
    x_wait(3, 4)
    z_step(7, 2)
    pass_on(1, 2)
    z_step(5, 2)
    z_step(6, 2)
    z_step(4, 2)
    pass_on(0)
    y_step(2)
    x_wait(1, 2)
    z_step(1, 1)
    z_step(2, 1)
    y_step(1)
    z_step(0, 1)
    z_step(3, 1)
    x_wait(0)
    back[2] = dot(m_own[...], gathered[0], ((1,), (0,))).astype(BF16)
    for part, out in ((0, grad_in), (1, grad_out)):
        acc = mine_t[part][c, y].astype(F32) + partner_t[part][y].astype(F32)
        for d in (0, 1):
            y_copy(d, 1, part).wait_recv()
            acc = acc + got_t[part][d, 0].astype(F32)
        out[...] = acc
    for tick in (1, 2, 0, 3):
        for d in (PLUS, MINUS):
            z_copy(d, tick).wait_recv()

    for k in range(8):
        for dx in (1, 2, 3):
            x_copy(k, dx).wait_send()
        pass_copy(k).wait_send()
    for part in (0, 1):
        c_copy(part).wait_send()
    for (d, hop), which in y_parts.items():
        for part in which:
            y_copy(d, hop, part).wait_send()
    for tick in range(TICKS):
        for d in (PLUS, MINUS):
            z_copy(d, tick).wait_send()


def collect(results, part_in, part_out, m_own, m_dirs):
    width = results.shape[1]
    n = m_own.shape[0]
    _, _, share, hidden = part_in.shape
    dma = pltpu.SemaphoreType.DMA
    shard_in, shard_out = (share, hidden), (hidden, share)
    return pl.pallas_call(
        collect_kernel,
        out_shape=(
            jax.ShapeDtypeStruct((3, n, width), BF16),
            jax.ShapeDtypeStruct(shard_in, F32),
            jax.ShapeDtypeStruct(shard_out, F32),
        ),
        in_specs=[pl.BlockSpec(memory_space=VMEM)] * 5,
        out_specs=(pl.BlockSpec(memory_space=VMEM),) * 3,
        scratch_shapes=[
            VMEM((8, NX * SLOTS, width), BF16),
            VMEM((8, SLOTS, width), BF16),
            VMEM((2, SUB * TICKS, width), BF16),
            VMEM((2, SUB * TICKS, width), BF16),
            VMEM((NY,) + shard_in, BF16), VMEM((NY,) + shard_out, BF16),
            VMEM((2, 4) + shard_in, BF16), VMEM((2, 4) + shard_out, BF16),
            VMEM((2, 4) + shard_in, BF16), VMEM((2, 4) + shard_out, BF16),
            dma((2, TICKS)), dma((2, TICKS)),
            dma((8, 3)), dma((8, 3)),
            dma((8,)), dma((8,)),
            dma((2, 4, 2)), dma((2, 4, 2)),
            dma((2,)), dma((2,)),
        ],
        compiler_params=pltpu.CompilerParams(collective_id=1, has_side_effects=True),
        name="collect",
    )(results, part_in, part_out, m_own, m_dirs)


def finish_kernel(back, perm_plus, perm_minus, sum_in, sum_out, grad_tokens, grad_gates, grad_in, grad_out):
    model = grad_tokens.shape[1]
    total = back[2].astype(F32)
    for d, perm in ((PLUS, perm_plus), (MINUS, perm_minus)):
        total = total + dot(perm[...], back[d], ((1,), (0,)))
    grad_tokens[...] = total[:, :model].astype(BF16)
    grad_gates[...] = total[:, model:].T[0:2, :].astype(BF16)
    grad_in[...] = sum_in[...]
    grad_out[...] = sum_out[...]


def finish(back, perm_plus, perm_minus, sum_in, sum_out):
    _, n, width = back.shape
    return pl.pallas_call(
        finish_kernel,
        out_shape=(
            jax.ShapeDtypeStruct((n, width - LANES), BF16),
            jax.ShapeDtypeStruct((2, n), BF16),
            jax.ShapeDtypeStruct(sum_in.shape, F32),
            jax.ShapeDtypeStruct(sum_out.shape, F32),
        ),
        in_specs=[pl.BlockSpec(memory_space=VMEM)] * 5,
        out_specs=(pl.BlockSpec(memory_space=VMEM),) * 4,
        name="finish",
    )(back, perm_plus, perm_minus, sum_in, sum_out)


def on_device(tokens, out_grad, route_ids, route_gates, weight_in, weight_out):
    own, plus, minus, perm_plus, perm_minus = prepare(tokens, out_grad, route_ids.T, route_gates.T)
    slots, full_in, full_out, m_own, m_dirs = dispatch(own, plus, minus, weight_in[0], weight_out[0])
    results, part_in, part_out = run_experts(slots, full_in, full_out)
    back, sum_in, sum_out = collect(results, part_in, part_out, m_own, m_dirs)
    grad_tokens, grad_gates, grad_in, grad_out = finish(back, perm_plus, perm_minus, sum_in, sum_out)
    return grad_tokens, grad_gates.T, grad_in[None], grad_out[None]


def solution(mesh):
    rows = P(("dp", "expert"), None)
    return jax.shard_map(
        on_device,
        mesh=mesh,
        in_specs=(rows, rows, rows, rows, P("expert", "dp", None), P("expert", None, "dp")),
        out_specs=(rows, rows, P("expert", "dp", None), P("expert", None, "dp")),
        check_vma=False,
    )
```
